512 devices in a mesh: dp: 32 (over x_hi, y, core), vocab: 16 (over z, x_lo).
Axes of the slice: x: 4 (x_hi: 2, x_lo: 2; x = x_hi * 2 + x_lo), y: 8, z: 8, core: 2. Of those that a mesh axis runs over, the one named last changes fastest.
Arguments:
- final_states: bfloat16 [65536, 5376], P(('dp', 'vocab')), may hold values from -12 to 12
- head_blocks: bfloat16 [16, 128, 5376], P('vocab'), may hold values from -0.17048273 to 0.17048273
- block_order: int32 [16], replicated, may hold values from 0 to 15, as said below
- row_tags: int32 [65536], P(('dp', 'vocab')), may hold values from 0 to 3, as said below
- target_word: int32 [65536], P(('dp', 'vocab')), may hold values from 0 to 511
- row_weight: bfloat16 [65536], P(('dp', 'vocab')), may hold values from 0.25 to 2
Outputs:
- row_loss: float32 [65536], P(('dp', 'vocab'))
- state_grad: bfloat16 [65536, 5376], P(('dp', 'vocab'))
- head_grad: float32 [16, 128, 5376], P('vocab', 'dp')
The draws below stay inside these ranges and needn't reach their ends.
Inputs may be any that keep to these rules, and one draw needn't show every extreme that they name: `row_tags`: among the rows of one device at most 40 carry any one tag; one tag, the same on every device, is carried by exactly 40 rows of each device. Each block number appears once; the shortlist of tag l is block_order[l * 4] to block_order[(l + 1) * 4 - 1].
All inputs are finite; a program needn't handle non-finite values.
Results may differ from the reference program's by a relative error of at most 0.0052.
Values may be sent and summed in bfloat16 or wider, within the bound.
No kernel may reach another device: no remote copies, remote signals or barrier semaphores. Data moves between devices by JAX's collectives and lax.ppermute only.
A program may use at most 128 MiB of HBM per device.

```python
import math
import jax
import jax.numpy as jnp
from jax import lax

D = 5376
BLOCK = 128
LANGS = 4
TOK_DEV = 128
CAP = 40
HEAD_BLOCKS = 16
SHORT_BLOCKS = 4
TOKENS = 65536


def layout_draw(key):
    block_perm = jax.random.permutation(jax.random.fold_in(key, 21), HEAD_BLOCKS).astype(jnp.int32)
    hot_tag = jax.random.randint(jax.random.fold_in(key, 22), (), 0, LANGS)
    device_keys = jax.random.split(jax.random.fold_in(key, 23), TOKENS // TOK_DEV)
    rest_rows = TOK_DEV - CAP

    def device_tags(dev_key):
        key_one, key_two, key_three, key_four = jax.random.split(dev_key, 4)
        count_one = jax.random.randint(key_one, (), max(0, rest_rows - 2 * CAP), min(CAP, rest_rows) + 1)
        remain = rest_rows - count_one
        count_two = jax.random.randint(key_two, (), jnp.maximum(0, remain - CAP), jnp.minimum(CAP, remain) + 1)
        count_three = remain - count_two
        others = jax.random.permutation(key_three, (hot_tag + 1 + jnp.arange(3, dtype=jnp.int32)) % LANGS)
        counts = jnp.zeros((LANGS,), jnp.int32).at[hot_tag].set(CAP)
        counts = counts.at[others[0]].set(count_one).at[others[1]].set(count_two).at[others[2]].set(count_three)
        bounds = jnp.cumsum(counts)
        sorted_tags = jnp.sum((jnp.arange(TOK_DEV, dtype=jnp.int32)[:, None] >= bounds[None, :]).astype(jnp.int32), axis=1)
        return jax.random.permutation(key_four, sorted_tags)
    tag_rows = jax.vmap(device_tags)(device_keys).reshape(-1).astype(jnp.int32)
    return (block_perm, tag_rows)


def head_table(key):
    normal_part = jax.random.truncated_normal(jax.random.fold_in(key, 31), -4.0, 4.0, (HEAD_BLOCKS, BLOCK, D), jnp.float32)
    return normal_part * (3.0 / math.sqrt(D))


def draw_head_blocks(key, part):
    return head_table(key).astype(jnp.bfloat16)


def draw_block_order(key, part):
    return layout_draw(key)[0]


def draw_row_tags(key, part):
    return layout_draw(key)[1]


def draw_final_states(key, part):
    return jax.random.truncated_normal(jax.random.fold_in(key, 41), -5.0, 5.0, (TOKENS, D), jnp.float32).astype(jnp.bfloat16)


def touch_ends(result, rng, least, top_value):
    longest = result.shape.index(max(result.shape))
    spots = []
    for shift in (0, 1):
        where = [jax.random.randint(jax.random.fold_in(rng, axis), (), 0, length) for axis, length in enumerate(result.shape)]
        where[longest] = (where[longest] + shift) % result.shape[longest]
        spots.append(tuple(where))
    return result.at[spots[0]].set(least).at[spots[1]].set(top_value)


def block_levels(stream_key, shape, shards, low, high):
    gain = 1.0
    for dim, shards_of in shards:
        heights = jax.random.uniform(jax.random.fold_in(jax.random.fold_in(stream_key, 6), dim), (shards_of,), jnp.float32, low / len(shards), high / len(shards))
        gain = gain * jnp.repeat(jnp.exp(heights), shape[dim] // shards_of).reshape((-1,) + (1,) * (len(shape) - 1 - dim))
    return gain


def setup_inputs(seed: int = 0) -> dict:
    seeds = jax.random.split(jax.random.key(seed), 7)
    return {
        "final_states": draw_final_states(jax.random.fold_in(seeds[6], 71), 0),
        "head_blocks": draw_head_blocks(jax.random.fold_in(seeds[6], 71), 0),
        "block_order": draw_block_order(jax.random.fold_in(seeds[6], 71), 0),
        "row_tags": draw_row_tags(jax.random.fold_in(seeds[6], 71), 0),
        "target_word": touch_ends(jax.random.randint(seeds[4], (TOKENS,), 0, SHORT_BLOCKS * BLOCK), jax.random.fold_in(seeds[4], 1), 0, (SHORT_BLOCKS * BLOCK) - 1).astype(jnp.int32),
        "row_weight": jnp.clip(0.25 + 1.75 * jax.random.uniform(seeds[5], (TOKENS,), jnp.float32) ** block_levels(seeds[5], (TOKENS,), ((0, 512),), -0.2, 0.2), 0.25, 2.0).astype(jnp.bfloat16),
    }


def reference(final_states, head_blocks, block_order, row_tags, target_word, row_weight):
    block_count = head_blocks.shape[0]
    short_len = block_count // LANGS
    model_width = head_blocks.shape[2]
    columns = block_count * BLOCK
    flat_head = head_blocks.reshape(columns, model_width)
    head_wide = head_blocks.astype(jnp.float32)
    block_ids = jnp.arange(block_count, dtype=jnp.int32)
    placed = jnp.sum(block_ids[:, None] * (block_order[:, None] == block_ids[None, :]).astype(jnp.int32), axis=0)
    owner_tag = placed // short_len
    column_ids = jnp.arange(columns, dtype=jnp.int32)
    column_owner = owner_tag[column_ids // BLOCK]
    row_block = 512
    block_steps = final_states.shape[0] // row_block

    def one_block(grad_total, block_items):
        states, tag_block, target, weight = block_items
        logits = jnp.dot(states, flat_head.T, preferred_element_type=jnp.float32)
        inside = column_owner[None, :] == tag_block[:, None]
        target_block = block_order[tag_block * short_len + target // BLOCK]
        target_col = target_block * BLOCK + target % BLOCK
        target_hit = column_ids[None, :] == target_col[:, None]
        row_peak = jnp.max(jnp.where(inside, logits, -1e30), axis=1)
        exp_total = jnp.sum(jnp.where(inside, jnp.exp(logits - row_peak[:, None]), 0.0), axis=1)
        log_total = row_peak + jnp.log(exp_total)
        picked = jnp.sum(jnp.where(target_hit, logits, 0.0), axis=1)
        row_losses = log_total - picked
        row_probs = jnp.exp(logits - log_total[:, None])
        slot_grads = jnp.where(inside, weight.astype(jnp.float32)[:, None] * (row_probs - target_hit.astype(jnp.float32)), 0.0).astype(jnp.bfloat16)
        grads_wide = slot_grads.astype(jnp.float32).reshape(-1, block_count, BLOCK)
        partial_value = jnp.einsum('rbw,bwd->rbd', grads_wide, head_wide).astype(jnp.bfloat16)
        partial_value = lax.optimization_barrier(partial_value)
        state_rows = jnp.sum(partial_value.astype(jnp.float32), axis=1).astype(jnp.bfloat16)
        grad_total = grad_total + jnp.einsum('rbw,rd->bwd', grads_wide, states.astype(jnp.float32))
        return grad_total, (row_losses, state_rows)

    block_items = (final_states.reshape(block_steps, row_block, model_width),
                   row_tags.reshape(block_steps, row_block),
                   target_word.reshape(block_steps, row_block),
                   row_weight.reshape(block_steps, row_block))
    start_grad = jnp.zeros((block_count, BLOCK, model_width), jnp.float32)
    head_grad, outputs = lax.scan(one_block, start_grad, block_items)
    row_loss = outputs[0].reshape(-1)
    state_grad = outputs[1].reshape(-1, model_width)
    return row_loss, state_grad, head_grad
```

```python
import jax
import jax.numpy as jnp
from jax import lax
from jax.sharding import Mesh, PartitionSpec as P

LANGS = 4
XH, Y, CORE = 2, 8, 2
Z, XL = 8, 2
DP = ("xh", "y", "core")
VOCAB = ("z", "xl")
F32 = jnp.float32
BF16 = jnp.bfloat16


def swap_all(value, axis):
    return lax.all_to_all(value, axis, split_axis=0, concat_axis=0, tiled=True)


def shards(final_states, head_blocks, block_order, row_tags, target_word, row_weight):
    rows, width = final_states.shape
    blocks = block_order.shape[0]
    words = head_blocks.shape[1]
    short = blocks // LANGS
    feats = width // Y
    wide = -(-feats // 128) * 128
    half_words = words // CORE
    group = rows * Y
    half_cols = short * half_words
    core = lax.axis_index("core")
    y_here = lax.axis_index("y")

    sliced = jnp.transpose(final_states.reshape(rows, Y, feats), (1, 0, 2))
    tag_lanes = jnp.broadcast_to(
        row_tags.astype(BF16)[None, :, None], (Y, rows, wide - feats)
    )
    states = swap_all(jnp.concatenate([sliced, tag_lanes], axis=2), "y").reshape(group, wide)

    own_words = lax.dynamic_index_in_dim(
        head_blocks[0].reshape(XH * Y, CORE, -1, width), core, axis=1, keepdims=False
    ).reshape(half_words, width)
    piece = lax.dynamic_slice_in_dim(own_words, y_here * feats, feats, axis=1)
    piece = jnp.pad(piece, ((0, 0), (0, wide - feats)))
    got_head = swap_all(jnp.broadcast_to(piece[None], (blocks, half_words, wide)), VOCAB)
    own_head = jnp.take(got_head, block_order, axis=0).reshape(blocks * half_words, wide)
    other_head = lax.ppermute(own_head, "core", [(0, 1), (1, 0)])

    tags = states[:, feats].astype(jnp.int32)
    tag_hit = [tags[:, None] == tag for tag in range(LANGS)]

    def pick(all_logits):
        picked = all_logits[:, :half_cols]
        for tag in range(1, LANGS):
            picked = jnp.where(
                tag_hit[tag], all_logits[:, tag * half_cols:(tag + 1) * half_cols], picked
            )
        return picked

    def logits_of(head):
        return pick(
            lax.dot_general(states, head, (((1,), (1,)), ((), ())), preferred_element_type=F32)
        )

    partial = jnp.concatenate([logits_of(own_head), logits_of(other_head)], axis=1)
    logits = jnp.sum(swap_all(partial.reshape(Y, rows, 2 * half_cols), "y"), axis=0)

    slot = target_word // words
    word = target_word % words
    fine = words // (XH * Y * CORE)
    word_core = word // fine % CORE
    word_rank = word // (fine * CORE) * fine + word % fine
    other_half = (word_core != core).astype(jnp.int32)
    position = other_half * half_cols + slot * half_words + word_rank
    target_hit = jnp.arange(2 * half_cols, dtype=jnp.int32)[None, :] == position[:, None]

    peak = jnp.max(logits, axis=1, keepdims=True)
    log_total = peak + jnp.log(jnp.sum(jnp.exp(logits - peak), axis=1, keepdims=True))
    row_loss = log_total[:, 0] - jnp.sum(jnp.where(target_hit, logits, 0.0), axis=1)
    grads = (
        row_weight.astype(F32)[:, None]
        * (jnp.exp(logits - log_total) - target_hit.astype(F32))
    ).astype(BF16)

    all_grads = swap_all(
        jnp.broadcast_to(grads[None], (Y, rows, 2 * half_cols)), "y"
    ).reshape(group, 2 * half_cols)

    def spread(part):
        zero = jnp.zeros((), BF16)
        return jnp.concatenate(
            [jnp.where(tag_hit[tag], part, zero) for tag in range(LANGS)], axis=1
        )

    own_grads = spread(all_grads[:, :half_cols])
    other_grads = spread(all_grads[:, half_cols:])

    def head_term(slot_grads):
        return lax.dot_general(
            slot_grads, states, (((0,), (0,)), ((), ())), preferred_element_type=F32
        )

    passed = lax.ppermute(head_term(other_grads).astype(BF16), "core", [(0, 1), (1, 0)])
    head_sum = (head_term(own_grads) + passed.astype(F32)).astype(BF16)
    block_ids = jnp.arange(blocks, dtype=jnp.int32)
    placed = jnp.sum(
        block_ids[:, None] * (block_order[:, None] == block_ids[None, :]).astype(jnp.int32), axis=0
    )
    by_block = jnp.take(head_sum.reshape(blocks, half_words, wide), placed, axis=0)
    got_terms = jnp.sum(swap_all(by_block, VOCAB).astype(F32), axis=0)[:, :feats]
    shares = swap_all(got_terms.reshape(XH * Y, fine, feats), ("xh", "y"))
    share = jnp.sum(shares.reshape(XH, Y, fine, feats), axis=0)
    head_share = jnp.transpose(share, (1, 0, 2)).reshape(1, fine, width)

    def state_term(slot_grads, head):
        return lax.dot_general(
            slot_grads, head, (((1,), (0,)), ((), ())), preferred_element_type=F32
        )

    state_part = (state_term(own_grads, own_head) + state_term(other_grads, other_head)).astype(BF16)
    state_back = swap_all(state_part.reshape(Y, rows, wide), "y")[:, :, :feats]
    state_grad = jnp.transpose(state_back, (1, 0, 2)).reshape(rows, width)
    return row_loss, state_grad, head_share


def solution(mesh):
    fine_mesh = Mesh(mesh.devices.reshape(XH, Y, CORE, Z, XL), DP + VOCAB)
    every = P(DP + VOCAB)
    return jax.shard_map(
        shards,
        mesh=fine_mesh,
        in_specs=(P(DP + VOCAB, None), P(VOCAB, None, None), P(), every, every, every),
        out_specs=(every, P(DP + VOCAB, None), P(VOCAB, DP, None)),
        check_vma=False,
    )
```

```python
import jax
import jax.numpy as jnp
from jax import lax
from jax.sharding import Mesh, PartitionSpec as P

LANGS = 4
XH, Y, CORE = 2, 8, 2
Z, XL = 8, 2
DP = ("xh", "y", "core")
VOCAB = ("z", "xl")
F32 = jnp.float32
BF16 = jnp.bfloat16


def swap_all(value, axis):
    return lax.all_to_all(value, axis, split_axis=0, concat_axis=0, tiled=True)


def reorder(value, index):
    return value.at[index].get(mode="promise_in_bounds")


def y_exchange(parts, y_here):
    got = [lax.dynamic_index_in_dim(parts, y_here, 0, keepdims=False)]
    for shift in range(1, Y):
        part = lax.dynamic_index_in_dim(parts, (y_here + shift) % Y, 0, keepdims=False)
        got.append(lax.ppermute(part, "y", [(j, (j + shift) % Y) for j in range(Y)]))
    return reorder(jnp.stack(got), (y_here - jnp.arange(Y, dtype=jnp.int32)) % Y)


def shards(final_states, head_blocks, block_order, row_tags, target_word, row_weight):
    rows, width = final_states.shape
    blocks = block_order.shape[0]
    words = head_blocks.shape[1]
    short = blocks // LANGS
    feats = width // Y
    wide = feats + 16
    half_words = words // CORE
    group = rows * Y
    half_cols = short * half_words
    core = lax.axis_index("core")
    y_here = lax.axis_index("y")

    sliced = jnp.transpose(final_states).reshape(Y, feats, rows)
    tag_feats = jnp.broadcast_to(row_tags.astype(BF16)[None, None, :], (Y, wide - feats, rows))
    got_states = y_exchange(jnp.concatenate([sliced, tag_feats], axis=1), y_here)
    states = jnp.transpose(got_states, (0, 2, 1)).reshape(group, wide)
    tags = got_states[:, feats, :].reshape(group).astype(jnp.int32)

    own_words = lax.dynamic_index_in_dim(
        head_blocks[0].reshape(XH * Y, CORE, -1, width), core, axis=1, keepdims=False
    ).reshape(half_words, width)
    piece = lax.dynamic_slice_in_dim(own_words, y_here * feats, feats, axis=1)
    piece = jnp.pad(piece, ((0, 0), (0, wide - feats)))
    got_head = swap_all(jnp.broadcast_to(piece[None], (blocks, half_words, wide)), VOCAB)
    own_head = reorder(got_head, block_order).reshape(blocks * half_words, wide)
    other_head = lax.ppermute(own_head, "core", [(0, 1), (1, 0)])

    tag_hit = [tags[:, None] == tag for tag in range(LANGS)]

    def pick(all_logits):
        picked = all_logits[:, :half_cols]
        for tag in range(1, LANGS):
            picked = jnp.where(
                tag_hit[tag], all_logits[:, tag * half_cols:(tag + 1) * half_cols], picked
            )
        return picked

    def logits_of(head):
        return pick(
            lax.dot_general(states, head, (((1,), (1,)), ((), ())), preferred_element_type=F32)
        )

    partial = jnp.concatenate([logits_of(own_head), logits_of(other_head)], axis=1)
    logits = jnp.sum(swap_all(partial.reshape(Y, rows, 2 * half_cols), "y"), axis=0)

    slot = target_word // words
    word = target_word % words
    fine = words // (XH * Y * CORE)
    word_core = word // fine % CORE
    word_rank = word // (fine * CORE) * fine + word % fine
    other_half = (word_core != core).astype(jnp.int32)
    position = other_half * half_cols + slot * half_words + word_rank
    target_hit = jnp.arange(2 * half_cols, dtype=jnp.int32)[None, :] == position[:, None]

    peak = jnp.max(logits, axis=1, keepdims=True)
    log_total = peak + jnp.log(jnp.sum(jnp.exp(logits - peak), axis=1, keepdims=True))
    row_loss = log_total[:, 0] - jnp.sum(jnp.where(target_hit, logits, 0.0), axis=1)
    grads = (
        row_weight.astype(F32)[:, None]
        * (jnp.exp(logits - log_total) - target_hit.astype(F32))
    ).astype(BF16)

    all_grads = swap_all(
        jnp.broadcast_to(grads[None], (Y, rows, 2 * half_cols)), "y"
    ).reshape(group, 2 * half_cols)

    def spread(part):
        zero = jnp.zeros((), BF16)
        return jnp.concatenate(
            [jnp.where(tag_hit[tag], part, zero) for tag in range(LANGS)], axis=1
        )

    own_grads = spread(all_grads[:, :half_cols])
    other_grads = spread(all_grads[:, half_cols:])

    def head_term(slot_grads):
        return lax.dot_general(
            slot_grads, states, (((0,), (0,)), ((), ())), preferred_element_type=F32
        )

    passed = lax.ppermute(head_term(other_grads).astype(BF16), "core", [(0, 1), (1, 0)])
    head_sum = (head_term(own_grads) + passed.astype(F32)).astype(BF16)
    block_ids = jnp.arange(blocks, dtype=jnp.int32)
    placed = jnp.sum(
        block_ids[:, None] * (block_order[:, None] == block_ids[None, :]).astype(jnp.int32), axis=0
    )
    by_block = reorder(head_sum.reshape(blocks, half_words, wide), placed)
    got_terms = jnp.sum(swap_all(by_block, VOCAB).astype(F32), axis=0)[:, :feats]
    shares = swap_all(got_terms.reshape(XH * Y, fine, feats), ("xh", "y"))
    share = jnp.sum(shares.reshape(XH, Y, fine, feats), axis=0)
    head_share = jnp.transpose(share, (1, 0, 2)).reshape(1, fine, width)

    def state_term(slot_grads, head):
        return lax.dot_general(
            slot_grads, head, (((1,), (0,)), ((), ())), preferred_element_type=F32
        )

    state_part = (state_term(own_grads, own_head) + state_term(other_grads, other_head)).astype(BF16)
    state_parts = jnp.transpose(state_part.reshape(Y, rows, wide), (0, 2, 1))[:, :feats]
    state_grad = jnp.transpose(y_exchange(state_parts, y_here).reshape(width, rows))
    return row_loss, state_grad, head_share


def solution(mesh):
    fine_mesh = Mesh(mesh.devices.reshape(XH, Y, CORE, Z, XL), DP + VOCAB)
    every = P(DP + VOCAB)
    return jax.shard_map(
        shards,
        mesh=fine_mesh,
        in_specs=(P(DP + VOCAB, None), P(VOCAB, None, None), P(), every, every, every),
        out_specs=(every, P(DP + VOCAB, None), P(VOCAB, DP, None)),
        check_vma=False,
    )
```

```python
import jax
import jax.numpy as jnp
from jax import lax
from jax.sharding import Mesh, PartitionSpec as P

LANGS = 4
XH, YH, YL, CORE = 2, 4, 2, 2
Z, XL = 8, 2
DP = ("xh", "yh", "yl", "core")
SPLIT = ("xh", "yl", "xl")
PARTS = XH * XL * YL
VOCAB = ("z", "xl")
F32 = jnp.float32
BF16 = jnp.bfloat16


def swap_all(value, axis):
    return lax.all_to_all(value, axis, split_axis=0, concat_axis=0, tiled=True)


def reorder(value, index):
    return value.at[index].get(mode="promise_in_bounds")


def exchange(parts, here):
    got = [lax.dynamic_index_in_dim(parts, here, 0, keepdims=False)]
    for flip in range(1, PARTS):
        part = lax.dynamic_index_in_dim(parts, here ^ flip, 0, keepdims=False)
        got.append(lax.ppermute(part, SPLIT, [(j, j ^ flip) for j in range(PARTS)]))
    return reorder(jnp.stack(got), here ^ jnp.arange(PARTS, dtype=jnp.int32))


def shards(final_states, head_blocks, block_order, row_tags, target_word, row_weight):
    rows, width = final_states.shape
    blocks = block_order.shape[0]
    words = head_blocks.shape[1]
    short = blocks // LANGS
    feats = width // PARTS
    wide = feats + 16
    half_words = words // CORE
    group = rows * PARTS
    half_cols = short * half_words
    fine = words // (XH * YH * YL * CORE)
    core = lax.axis_index("core")
    here = lax.axis_index(SPLIT)

    sliced = jnp.transpose(final_states).reshape(PARTS, feats, rows)
    tag_feats = jnp.broadcast_to(row_tags.astype(BF16)[None, None, :], (PARTS, wide - feats, rows))
    got_states = exchange(jnp.concatenate([sliced, tag_feats], axis=1), here)
    states = jnp.transpose(got_states, (0, 2, 1)).reshape(group, wide)
    tags = got_states[:, feats, :].reshape(group).astype(jnp.int32)

    first = lax.axis_index(("xh", "yl")) * XL

    def piece_for(xl):
        part = lax.dynamic_slice_in_dim(head_blocks[0], (first + xl) * feats, feats, axis=1)
        part = lax.dynamic_index_in_dim(
            part.reshape(half_words // fine, CORE, fine, feats), core, axis=1, keepdims=False
        )
        return jnp.pad(part.reshape(half_words, feats), ((0, 0), (0, wide - feats)))

    pieces = jnp.stack([piece_for(xl) for xl in range(XL)])
    got_head = swap_all(
        jnp.broadcast_to(pieces[None], (Z, XL, half_words, wide)).reshape(blocks, half_words, wide),
        VOCAB,
    )
    own_head = reorder(got_head, block_order).reshape(blocks * half_words, wide)
    other_head = lax.ppermute(own_head, "core", [(0, 1), (1, 0)])

    tag_hit = [tags[:, None] == tag for tag in range(LANGS)]

    def pick(all_logits):
        picked = all_logits[:, :half_cols]
        for tag in range(1, LANGS):
            picked = jnp.where(
                tag_hit[tag], all_logits[:, tag * half_cols:(tag + 1) * half_cols], picked
            )
        return picked

    def logits_of(head):
        return pick(
            lax.dot_general(states, head, (((1,), (1,)), ((), ())), preferred_element_type=F32)
        )

    partial = jnp.concatenate([logits_of(own_head), logits_of(other_head)], axis=1)
    logits = jnp.sum(swap_all(partial.reshape(PARTS, rows, 2 * half_cols), SPLIT), axis=0)

    slot = target_word // words
    word = target_word % words
    word_core = word // fine % CORE
    word_rank = word // (fine * CORE) * fine + word % fine
    other_half = (word_core != core).astype(jnp.int32)
    position = other_half * half_cols + slot * half_words + word_rank
    target_hit = jnp.arange(2 * half_cols, dtype=jnp.int32)[None, :] == position[:, None]

    peak = jnp.max(logits, axis=1, keepdims=True)
    log_total = peak + jnp.log(jnp.sum(jnp.exp(logits - peak), axis=1, keepdims=True))
    row_loss = log_total[:, 0] - jnp.sum(jnp.where(target_hit, logits, 0.0), axis=1)
    grads = (
        row_weight.astype(F32)[:, None]
        * (jnp.exp(logits - log_total) - target_hit.astype(F32))
    ).astype(BF16)

    all_grads = swap_all(
        jnp.broadcast_to(grads[None], (PARTS, rows, 2 * half_cols)), SPLIT
    ).reshape(group, 2 * half_cols)

    def spread(part):
        zero = jnp.zeros((), BF16)
        return jnp.concatenate(
            [jnp.where(tag_hit[tag], part, zero) for tag in range(LANGS)], axis=1
        )

    own_grads = spread(all_grads[:, :half_cols])
    other_grads = spread(all_grads[:, half_cols:])

    def head_term(slot_grads):
        return lax.dot_general(
            slot_grads, states, (((0,), (0,)), ((), ())), preferred_element_type=F32
        )

    passed = lax.ppermute(head_term(other_grads).astype(BF16), "core", [(0, 1), (1, 0)])
    head_sum = (head_term(own_grads) + passed.astype(F32)).astype(BF16)
    block_ids = jnp.arange(blocks, dtype=jnp.int32)
    placed = jnp.sum(
        block_ids[:, None] * (block_order[:, None] == block_ids[None, :]).astype(jnp.int32), axis=0
    )
    by_block = reorder(head_sum.reshape(blocks, half_words, wide), placed)
    got_terms = swap_all(by_block, VOCAB).astype(F32).reshape(Z, XL, half_words, wide)
    terms = jnp.sum(got_terms, axis=0)[:, :, :feats]
    outgoing = jnp.transpose(terms.reshape(XL, XH * YH * YL, fine, feats), (1, 0, 2, 3))
    shares = swap_all(outgoing, ("xh", "yh", "yl"))
    share = jnp.sum(shares.reshape(XH, YH, YL, XL, fine, feats), axis=1)
    head_share = jnp.transpose(share, (3, 0, 1, 2, 4)).reshape(1, fine, width)

    def state_term(slot_grads, head):
        return lax.dot_general(
            slot_grads, head, (((1,), (0,)), ((), ())), preferred_element_type=F32
        )

    state_part = (state_term(own_grads, own_head) + state_term(other_grads, other_head)).astype(BF16)
    state_parts = jnp.transpose(state_part.reshape(PARTS, rows, wide), (0, 2, 1))[:, :feats]
    state_grad = jnp.transpose(exchange(state_parts, here).reshape(width, rows))
    return row_loss, state_grad, head_share


def solution(mesh):
    fine_mesh = Mesh(mesh.devices.reshape(XH, YH, YL, CORE, Z, XL), DP + VOCAB)
    every = P(DP + VOCAB)
    return jax.shard_map(
        shards,
        mesh=fine_mesh,
        in_specs=(P(DP + VOCAB, None), P(VOCAB, None, None), P(), every, every, every),
        out_specs=(every, P(DP + VOCAB, None), P(VOCAB, DP, None)),
        check_vma=False,
    )
```
